512 devices in a mesh: seq: 256 (over z, x, y_hi, core), head: 2 (over y_lo).
Axes of the slice: x: 4, y: 8 (y_hi: 4, y_lo: 2; y = y_hi * 2 + y_lo), z: 8, core: 2. Of those that a mesh axis runs over, the one named last changes fastest.
Arguments:
- queries: bfloat16 [65536, 1792], P('seq', 'head'), may hold values from -120 to 120
- key_rows: bfloat16 [65536, 256], P('seq', 'head'), may hold values from -9 to 9
- value_rows: bfloat16 [65536, 256], P('seq', 'head'), may hold values from -6 to 6
- out_weight: bfloat16 [1792, 3584], P('head', 'seq'), may hold values from -0.125 to 0.125
Outputs:
- projected: bfloat16 [65536, 3584], P('seq', 'head')
The draws below stay inside these ranges and needn't reach their ends.
All inputs are finite; a program needn't handle non-finite values.
Results may differ from the reference program's by a relative error of at most 0.009.
Values may be sent and summed in bfloat16 or wider, within the bound.
A program may use at most 64 MiB of HBM per device.

```python
import math
import jax
import jax.numpy as jnp
from jax import lax

D = 3584
KVH = 2
QPK = 7
HD = 128
BLK = 256
TOKENS = 65536


def base_keys(key):
    normal_draw = jax.random.normal(jax.random.fold_in(key, 7101), (TOKENS, KVH * HD), jnp.float32)
    return jnp.clip(1.5 * normal_draw, -9.0, 9.0)


def draw_key_rows(key, part):
    keys_drawn = base_keys(key)
    return keys_drawn.astype(jnp.bfloat16)


def draw_queries(key, part):
    normal_draw = jax.random.normal(jax.random.fold_in(key, 7202), (TOKENS, KVH, QPK, HD), jnp.float32)
    drawn = jnp.clip(1.5 * normal_draw, -9.0, 9.0)
    return drawn.reshape(TOKENS, KVH * QPK * HD).astype(jnp.bfloat16)


def level_of(own_key, shape, cuts, low, largest):
    def one(axis_at, shards_of):
        heights = jax.random.uniform(jax.random.fold_in(jax.random.fold_in(own_key, 6), axis_at), (shards_of,), jnp.float32, low / len(cuts), largest / len(cuts))
        return jnp.repeat(jnp.exp(heights), shape[axis_at] // shards_of).reshape((-1,) + (1,) * (len(shape) - axis_at - 1))

    loudness = one(*cuts[0])
    for cut in cuts[1:]:
        loudness = loudness * one(*cut)
    return loudness


def bell_draw(own_key, shape, deviation, reach, cuts=(), kind=jnp.bfloat16):
    values = deviation * jax.random.normal(own_key, shape, jnp.float32)
    if cuts:
        values = values * level_of(own_key, shape, cuts, -0.22, 0.18)
    return jnp.clip(values, -reach, reach).astype(kind)


def setup_inputs(seed: int = 0) -> dict:
    keys = jax.random.split(jax.random.key(seed), 5)
    queries = draw_queries(jax.random.fold_in(keys[4], 71), 0)
    key_rows = draw_key_rows(jax.random.fold_in(keys[4], 71), 0)
    value_rows = bell_draw(keys[2], (TOKENS, KVH * HD), 1.0, 6.0, ((0, 256), (1, 2)))
    out_weight = bell_draw(keys[3], (KVH * QPK * HD, D), (KVH * QPK * HD) ** -0.5, 0.125, ((0, 2), (1, 256)))
    return {"queries": queries, "key_rows": key_rows, "value_rows": value_rows, "out_weight": out_weight}


def reference(queries, key_rows, value_rows, out_weight):
    block_count = TOKENS // BLK
    levels = block_count.bit_length() - 1
    score_scale = 1.0 / math.sqrt(HD)
    query_all = queries.reshape(block_count, BLK, KVH, QPK, HD)
    key_all = key_rows.reshape(block_count, BLK, KVH, HD)
    value_all = value_rows.reshape(block_count, BLK, KVH, HD)
    flip_masks = jnp.array([1 << level for level in range(1, levels)], dtype=jnp.int32)

    def one_block(block_number):
        beside_all = jnp.stack([block_number - 1, block_number, block_number + 1]).astype(jnp.int32)
        chosen = jnp.concatenate([beside_all, jnp.bitwise_xor(block_number, flip_masks).astype(jnp.int32)])
        usable = jnp.concatenate([jnp.stack([block_number > 0, block_number >= 0, block_number < block_count - 1]), jnp.ones(flip_masks.shape, dtype=bool)])
        clipped = jnp.clip(chosen, 0, block_count - 1).astype(jnp.int32)
        key_sel = key_all[clipped].reshape(-1, KVH, HD).astype(jnp.float32)
        value_sel = value_all[clipped].reshape(-1, KVH, HD).astype(jnp.float32)
        key_usable = jnp.repeat(usable, BLK)
        query_sel = query_all[block_number].astype(jnp.float32)
        scores = jnp.einsum('thqd,shd->hqts', query_sel, key_sel) * score_scale
        scores = jnp.where(key_usable, scores, -1e+30)
        peak = lax.optimization_barrier(jnp.max(scores, axis=-1, keepdims=True))
        weights = jnp.exp(scores - peak)
        weight_sum = lax.optimization_barrier(jnp.sum(weights, axis=-1))
        rounded = lax.optimization_barrier(weights.astype(jnp.bfloat16)).astype(jnp.float32)
        numerator = jnp.einsum('hqts,shd->thqd', rounded, value_sel)
        blended = numerator / jnp.transpose(weight_sum, (2, 0, 1))[..., None]
        attended = blended.astype(jnp.bfloat16).reshape(BLK, KVH * QPK * HD)
        return jnp.dot(attended, out_weight, preferred_element_type=jnp.float32).astype(jnp.bfloat16)
    result = lax.map(one_block, jnp.arange(block_count, dtype=jnp.int32))
    return result.reshape(TOKENS, D)
```

```python
import functools
import math

import jax
import jax.numpy as jnp
from jax import lax
from jax.experimental import pallas as pl
from jax.experimental.pallas import tpu as pltpu
from jax.sharding import PartitionSpec as P

QPK = 7
HD = 128
BLK = 256
MESH = pl.DeviceIdType.MESH
NZ, NX, NY, NC = 4, 8, 4, 2
SEQ = NZ * NX * NY * NC
BITS = 8
SLOTS = BITS + 2
SHARD = 14
PACK = SHARD * NY * NC
ROWS = QPK * HD
FAR = 3


def body(
    q_hbm, k_hbm, v_hbm, w_hbm, out_ref,
    q_ref, kbuf, vbuf, shards, wbuf, s_ref, att, acc,
    load_sem, kv_send, kv_recv, sh_send, sh_recv, x_send, x_recv, xm_send, xm_recv,
    z_send, z_recv, zm_send, zm_recv, f_send, f_recv, fm_send, fm_recv, a_send, a_recv,
):
    seq = lax.axis_index("seq")
    head = lax.axis_index("head")
    core = seq % NC
    yh = (seq // NC) % NY
    x = (seq // (NC * NY)) % NX
    z = seq // (NC * NY * NX)
    d = 1 - 2 * core
    keep = (z // 2 + head) % 2 == 0

    def at(zz, xx, yy, cc):
        return ((zz % NZ * NX + xx % NX) * NY + yy % NY) * NC + cc % NC

    def flip(j):
        return seq + 2**j * (1 - 2 * ((seq // 2**j) % 2))

    kv_to = [(seq + 1) % SEQ, seq, (seq + SEQ - 1) % SEQ] + [flip(j) for j in range(1, BITS)]
    mate = at(z, x, yh, core + 1)
    x_next, x_prev = at(z, x + d + NX, yh, core), at(z, x - d + NX, yh, core)
    z_next, z_prev = at(z + d + NZ, x, yh, core), at(z - d + NZ, x, yh, core)

    away = 1 - ((z // 2 + head + 1) % 2)
    z_to = (z + 2 * away) % NZ
    head_to = (head + away) % 2
    sh_to = [at(z_to, x, yh + i // 2, core + i) for i in range(NY * NC)]

    loads = [
        pltpu.make_async_copy(q_hbm, q_ref, load_sem.at[0]),
        pltpu.make_async_copy(k_hbm, kbuf.at[1], load_sem.at[1]),
        pltpu.make_async_copy(v_hbm, vbuf.at[1], load_sem.at[2]),
    ]
    for copy in loads:
        copy.start()

    barrier = pltpu.get_barrier_semaphore()

    def greet(s, h):
        pl.semaphore_signal(barrier, inc=1, device_id=(s, h), device_id_type=MESH)

    for i in range(SLOTS):
        if i != 1:
            greet(kv_to[i], head)
    for s in (x_next, x_prev, z_next, z_prev):
        greet(s, head)
    greet(seq, 1 - head)
    for i in range(1, NY * NC):
        greet(sh_to[i], head_to)

    @pl.when(jnp.logical_not(keep))
    def _():
        greet(sh_to[0], head_to)

    pl.semaphore_wait(barrier, SLOTS - 1 + 5 + NY * NC - 1 + away)

    sent = []

    def remote(src, dst, send, recv, s, h=head):
        return pltpu.make_async_remote_copy(
            src_ref=src, dst_ref=dst, send_sem=send, recv_sem=recv, device_id=(s, h), device_id_type=MESH
        )

    def send(*args):
        copy = remote(*args)
        copy.start()
        sent.append(copy)

    mine = yh * NC + core
    sh_self = remote(w_hbm, shards.at[mine], sh_send.at[0], sh_recv.at[mine], sh_to[0], head_to)
    for i in range(1, NY * NC):
        send(w_hbm, shards.at[mine], sh_send.at[i], sh_recv.at[mine], sh_to[i], head_to)

    @pl.when(keep)
    def _():
        pltpu.make_async_copy(w_hbm, shards.at[mine], sh_recv.at[mine]).start()

    @pl.when(jnp.logical_not(keep))
    def _():
        sh_self.start()

    order = [0, 2, 3, 4, 5, 6, 7, 8, 9]
    for i in order:
        send(k_hbm, kbuf.at[i], kv_send.at[i, 0], kv_recv.at[i, 0], kv_to[i])
        send(v_hbm, vbuf.at[i], kv_send.at[i, 1], kv_recv.at[i, 1], kv_to[i])

    def chunk(zz, xx):
        zz = zz % NZ
        return wbuf.at[((zz // 2 + head) % 2) * 2 + zz % 2, xx % NX]

    def rel(a, dd):
        return [0, -dd, dd, -2 * dd, 2 * dd, -3 * dd, 3 * dd, 4][a] + x + NX

    def send_x(t):
        c = chunk(z, x - d * t + NX)
        send(c, c, x_send.at[t], x_recv.at[t], x_next)

    def wait_x(t):
        c = chunk(z, x - d * (t + 1) + NX)
        remote(c, c, x_send.at[t], x_recv.at[t], x_next).wait_recv()
        return c

    def mate_x(t):
        c = chunk(z, x - d * (t + 1) + NX)
        send(c, c, xm_send.at[t], xm_recv.at[t], mate)

    def wait_xm(t):
        c = chunk(z, x + d * (t + 1) + NX)
        remote(c, c, xm_send.at[t], xm_recv.at[t], mate).wait_recv()

    def send_z(a):
        c = chunk(z, rel(a, d))
        send(c, c, z_send.at[a], z_recv.at[a], z_next)

    def far_chunk(f, cc, dd):
        return x + 4 * cc if f == 0 else x - f * dd + NX

    def step_z(a):
        c = chunk(z - d + NZ, rel(a, d))
        remote(c, c, z_send.at[a], z_recv.at[a], z_next).wait_recv()
        if a in (1, 3, 5):
            f = (a + 1) // 2
            send(c, c, f_send.at[f], f_recv.at[f], z_next)
        if a in (0, 7):
            @pl.when(core == a // 7)
            def _():
                remote(c, c, f_send.at[0], f_recv.at[0], z_next).start()
        send(c, c, zm_send.at[a], zm_recv.at[a], mate)

    def wait_zm(a):
        c = chunk(z + d + NZ, rel(a, -d))
        remote(c, c, zm_send.at[a], zm_recv.at[a], mate).wait_recv()

    def step_f(f):
        c = chunk(z + 2, far_chunk(f, core, d))
        remote(c, c, f_send.at[f], f_recv.at[f], z_next).wait_recv()
        send(c, c, fm_send.at[f], fm_recv.at[f], mate)

    def wait_fm(f):
        c = chunk(z + 2, far_chunk(f, 1 - core, -d))
        remote(c, c, fm_send.at[f], fm_recv.at[f], mate).wait_recv()

    rate = (1.0 / math.sqrt(HD)) * math.log2(math.e)
    low = jnp.where(seq > 0, 3e38, -1e30).astype(jnp.float32)
    high = jnp.where(seq < SEQ - 1, 3e38, -1e30).astype(jnp.float32)

    def attend(h):
        cols = pl.ds(h * HD, HD)
        query = q_ref[:, cols]
        best = None
        for i in range(SLOTS):
            s = lax.dot_general(
                query, kbuf[i], (((1,), (1,)), ((), ())), preferred_element_type=jnp.float32
            )
            if i == 0:
                s = jnp.minimum(s, low)
            if i == 2:
                s = jnp.minimum(s, high)
            s_ref[:, i * BLK : (i + 1) * BLK] = s
            top = jnp.maximum(s[:, :HD], s[:, HD:])
            best = top if best is None else jnp.maximum(best, top)
        peak = jnp.max(best, axis=1, keepdims=True)
        total = jnp.zeros((BLK, HD), jnp.float32)
        blended = jnp.zeros((BLK, HD), jnp.float32)
        for i in range(SLOTS):
            w = jnp.exp2((s_ref[:, i * BLK : (i + 1) * BLK] - peak) * rate)
            total = total + w[:, :HD] + w[:, HD:]
            blended = blended + jnp.dot(
                w.astype(jnp.bfloat16), vbuf[i], preferred_element_type=jnp.float32
            )
        weight_sum = jnp.sum(total, axis=1, keepdims=True)
        att[0, :, cols] = (blended / weight_sum).astype(jnp.bfloat16)
        send(
            att.at[0, :, cols], att.at[1, :, cols], a_send.at[h], a_recv.at[h], seq, 1 - head
        )

    def wait_att(h):
        cols = pl.ds(h * HD, HD)
        remote(
            att.at[0, :, cols], att.at[1, :, cols], a_send.at[h], a_recv.at[h], seq, 1 - head
        ).wait_recv()

    def project(zz, first):
        zz = zz % NZ
        side = (zz // 2 + head) % 2
        w = wbuf[side * 2 + zz % 2].reshape(NX * PACK, ROWS)
        part = lax.dot_general(
            att[side], w, (((1,), (1,)), ((), ())), preferred_element_type=jnp.float32
        )
        if first:
            acc[zz % 2] = part
        else:
            acc[zz % 2] = acc[zz % 2] + part

    for i in range(NY * NC):
        remote(w_hbm, shards.at[i], sh_send.at[0], sh_recv.at[i], sh_to[0], head_to).wait_recv()
    own = chunk(z, x)
    rows = [shards[i].astype(jnp.float32) for i in range(NY * NC)]
    own[...] = jnp.concatenate(rows, axis=0).astype(jnp.bfloat16)

    def wait_kv(i):
        remote(k_hbm, kbuf.at[i], kv_send.at[i, 0], kv_recv.at[i, 0], kv_to[i]).wait_recv()
        remote(v_hbm, vbuf.at[i], kv_send.at[i, 1], kv_recv.at[i, 1], kv_to[i]).wait_recv()

    send_x(0)
    send_z(0)

    def hop_x(t):
        wait_x(t)
        if t < FAR:
            send_x(t + 1)
            mate_x(t)
            send_z(2 * t + 1)
        else:
            send_z(7)

    def side_x(t):
        wait_xm(t)
        send_z(2 * t + 2)

    for copy in loads:
        copy.wait()
    hop_x(0)
    side_x(0)
    step_z(0)
    hop_x(1)
    side_x(1)
    for i in order:
        wait_kv(i)
    attend(0)
    step_z(1)
    hop_x(2)
    side_x(2)
    attend(1)
    step_z(2)
    hop_x(3)
    attend(2)
    step_z(3)
    step_z(4)
    attend(3)
    step_z(5)
    attend(4)
    step_z(6)
    step_z(7)
    attend(5)
    step_f(1)
    attend(6)
    for h in range(QPK):
        wait_att(h)
    project(z, True)
    step_f(2)
    for a in range(8):
        wait_zm(a)
    project(z - d + NZ, True)
    step_f(3)
    step_f(0)
    project(z + d + NZ, False)
    for f in range(4):
        wait_fm(f)
    project(z + 2, False)
    out_ref[:, : NX * PACK] = acc[0].astype(jnp.bfloat16)
    out_ref[:, NX * PACK :] = acc[1].astype(jnp.bfloat16)

    for copy in sent:
        copy.wait_send()
    c = chunk(z - d + NZ, x + 4 * core)
    remote(c, c, f_send.at[0], f_recv.at[0], z_next).wait_send()

    @pl.when(jnp.logical_not(keep))
    def _():
        sh_self.wait_send()


def local(queries, key_rows, value_rows, out_weight):
    dma = pltpu.SemaphoreType.DMA
    f32, bf16 = jnp.float32, jnp.bfloat16
    shard_count = NY * NC
    return pl.pallas_call(
        body,
        out_shape=jax.ShapeDtypeStruct((BLK, 2 * NX * PACK), bf16),
        in_specs=[pl.BlockSpec(memory_space=pl.ANY)] * 4,
        out_specs=pl.BlockSpec(memory_space=pltpu.VMEM),
        scratch_shapes=[
            pltpu.VMEM((BLK, ROWS), bf16),
            pltpu.VMEM((SLOTS, BLK, HD), bf16),
            pltpu.VMEM((SLOTS, BLK, HD), bf16),
            pltpu.VMEM((shard_count, SHARD, ROWS), bf16),
            pltpu.VMEM((NZ, NX, PACK, ROWS), bf16),
            pltpu.VMEM((BLK, SLOTS * BLK), f32),
            pltpu.VMEM((2, BLK, ROWS), bf16),
            pltpu.VMEM((2, BLK, NX * PACK), f32),
            dma((3,)),
            dma((SLOTS, 2)), dma((SLOTS, 2)),
            dma((shard_count,)), dma((shard_count,)),
            dma((4,)), dma((4,)), dma((3,)), dma((3,)),
            dma((8,)), dma((8,)), dma((8,)), dma((8,)),
            dma((4,)), dma((4,)), dma((4,)), dma((4,)),
            dma((QPK,)), dma((QPK,)),
        ],
        compiler_params=pltpu.CompilerParams(
            collective_id=0, has_side_effects=True, vmem_limit_bytes=48 * 2**20
        ),
    )(queries, key_rows, value_rows, out_weight.T)


def solution(mesh):
    in_specs = (P("seq", "head"), P("seq", "head"), P("seq", "head"), P("head", "seq"))
    out_specs = P("seq", "head")
    return jax.shard_map(local, mesh=mesh, in_specs=in_specs, out_specs=out_specs, check_vma=False)
```

```python
import functools
import math

import jax
import jax.numpy as jnp
from jax import lax
from jax.experimental import pallas as pl
from jax.experimental.pallas import tpu as pltpu
from jax.sharding import PartitionSpec as P

QPK = 7
HD = 128
BLK = 256
MESH = pl.DeviceIdType.MESH
NZ, NX, NY, NC = 8, 4, 4, 2
HALF = NZ // 2
SEQ = NZ * NX * NY * NC
BITS = 8
SLOTS = BITS + 2
SHARD = 14
PACK = SHARD * NY * NC
ROWS = QPK * HD
FAR = 3
CUT = 5 * HD


def body(
    q_hbm, k_hbm, v_hbm, w_hbm, out_ref,
    q_ref, kbuf, vbuf, shards, wbuf, s_ref, att, acc,
    load_sem, kv_send, kv_recv, sh_send, sh_recv, z_send, z_recv, zm_send, zm_recv,
    x_send, x_recv, xm_send, xm_recv, f_send, f_recv, fm_send, fm_recv,
    q_send, q_recv, qm_send, qm_recv, t_send, t_recv, tm_send, tm_recv, a_send, a_recv,
):
    seq = lax.axis_index("seq")
    head = lax.axis_index("head")
    core = seq % NC
    yh = (seq // NC) % NY
    x = (seq // (NC * NY)) % NX
    z = seq // (NC * NY * NX)
    d = 1 - 2 * core
    keep = (z // HALF + head) % 2 == 0

    def at(zz, xx, yy, cc):
        return ((zz % NZ * NX + xx % NX) * NY + yy % NY) * NC + cc % NC

    def flip(j):
        return seq + 2**j * (1 - 2 * ((seq // 2**j) % 2))

    kv_to = [(seq + 1) % SEQ, seq, (seq + SEQ - 1) % SEQ] + [flip(j) for j in range(1, BITS)]
    mate = at(z, x, yh, core + 1)
    x_next, x_prev = at(z, x + d + NX, yh, core), at(z, x - d + NX, yh, core)
    z_next, z_prev = at(z + d + NZ, x, yh, core), at(z - d + NZ, x, yh, core)
    z_next2, z_prev2 = at(z + 2 * d + NZ, x, yh, core), at(z - 2 * d + NZ, x, yh, core)
    x_far = at(z, x + 2, yh, core)

    away = (z // HALF + head) % 2
    z_to = z + away * (NZ - 1 - 2 * z)
    head_to = (head + away) % 2
    sh_to = [at(z_to, x, yh + i // 2, core + i) for i in range(NY * NC)]

    loads = [
        pltpu.make_async_copy(q_hbm, q_ref, load_sem.at[0]),
        pltpu.make_async_copy(k_hbm, kbuf.at[1], load_sem.at[1]),
        pltpu.make_async_copy(v_hbm, vbuf.at[1], load_sem.at[2]),
    ]
    for copy in loads:
        copy.start()

    barrier = pltpu.get_barrier_semaphore()

    def greet(s, h):
        pl.semaphore_signal(barrier, inc=1, device_id=(s, h), device_id_type=MESH)

    for i in range(SLOTS):
        if i != 1:
            greet(kv_to[i], head)
    for s in (x_next, x_prev, z_next, z_prev, z_next2, z_prev2):
        greet(s, head)
    greet(seq, 1 - head)
    for i in range(1, NY * NC):
        greet(sh_to[i], head_to)

    @pl.when(jnp.logical_not(keep))
    def _():
        greet(sh_to[0], head_to)

    pl.semaphore_wait(barrier, SLOTS - 1 + 7 + NY * NC - 1 + away)

    sent = []

    def remote(src, dst, send, recv, s, h=head):
        return pltpu.make_async_remote_copy(
            src_ref=src, dst_ref=dst, send_sem=send, recv_sem=recv, device_id=(s, h), device_id_type=MESH
        )

    def send(*args):
        copy = remote(*args)
        copy.start()
        sent.append(copy)

    mine = yh * NC + core
    sh_self = remote(w_hbm, shards.at[mine], sh_send.at[0], sh_recv.at[mine], sh_to[0], head_to)
    for i in range(1, NY * NC):
        send(w_hbm, shards.at[mine], sh_send.at[i], sh_recv.at[mine], sh_to[i], head_to)

    @pl.when(keep)
    def _():
        pltpu.make_async_copy(w_hbm, shards.at[mine], sh_recv.at[mine]).start()

    @pl.when(jnp.logical_not(keep))
    def _():
        sh_self.start()

    order = [0, 2, 3, 4, 5, 6, 7, 8, 9]
    for i in order:
        send(k_hbm, kbuf.at[i], kv_send.at[i, 0], kv_recv.at[i, 0], kv_to[i])
        send(v_hbm, vbuf.at[i], kv_send.at[i, 1], kv_recv.at[i, 1], kv_to[i])

    def place(zz):
        side = ((zz % NZ) // HALF + head) % 2
        quarter = zz % HALF
        return side, quarter + side * (HALF - 1 - 2 * quarter)

    def chunk(zz, xx):
        side, quarter = place(zz)
        return wbuf.at[xx % NX, side, quarter, :, pl.ds(0, CUT)]

    def whole(zz, xx):
        side, quarter = place(zz)
        return wbuf.at[xx % NX, side, quarter]

    def tail(zz, xx):
        side, quarter = place(zz)
        return wbuf.at[xx % NX, side, quarter, :, pl.ds(CUT, ROWS - CUT)]

    def half_tail(zz, xx, cc):
        side, quarter = place(zz)
        lanes = pl.ds(pl.multiple_of(CUT + HD * cc, HD), HD)
        return wbuf.at[xx % NX, side, quarter, :, lanes]

    def tail_row(zz):
        side, quarter = place(zz)
        return wbuf.at[:, side, quarter, :, pl.ds(CUT, ROWS - CUT)]

    def rel(a, dd):
        return [0, -dd, dd, -2 * dd, 2 * dd, -3 * dd, 3 * dd, 4][a] + z + NZ

    even = z % 2 == core

    def z_copy(t, c):
        to = (z_next, z_next2, z_next, z_next2)[t]
        return remote(c, c, z_send.at[t], z_recv.at[t], to)

    def send_z(t):
        copy = z_copy(t, chunk(z, x))
        copy.start()
        sent.append(copy)

    def z_mate(t):
        c = chunk(z - d * (t + 1) + NZ, x)
        return remote(c, c, zm_send.at[t], zm_recv.at[t], mate)

    def hop_z(t):
        c = chunk(z - d * (t + 1) + NZ, x)
        if t == FAR:
            @pl.when(even)
            def _():
                z_copy(t, c).wait_recv()
                z_mate(t).start()

            return
        z_copy(t, c).wait_recv()
        if t == 1:
            @pl.when(even)
            def _():
                z_copy(3, c).start()

            copy = z_copy(2, c)
            copy.start()
            sent.append(copy)
        copy = z_mate(t)
        copy.start()
        sent.append(copy)
        send_x(2 * t + 1)

    def side_z(t):
        c = chunk(z + d * (t + 1) + NZ, x)
        copy = remote(c, c, zm_send.at[t], zm_recv.at[t], mate)
        if t == FAR:
            @pl.when(jnp.logical_not(even))
            def _():
                copy.wait_recv()

            send_x(7)
        else:
            copy.wait_recv()
            send_x(2 * t + 2)

    def send_x(a):
        c = chunk(rel(a, d), x)
        send(c, c, x_send.at[a], x_recv.at[a], x_next)

    def far_chunk(f, cc, dd):
        return z + 4 * cc if f == 0 else z - f * dd + NZ

    def step_x(a):
        c = chunk(rel(a, d), x - d + NX)
        remote(c, c, x_send.at[a], x_recv.at[a], x_next).wait_recv()
        if a in (1, 3, 5):
            f = (a + 1) // 2
            send(c, c, f_send.at[f], f_recv.at[f], x_next)
        if a in (0, 7):
            @pl.when(core == a // 7)
            def _():
                remote(c, c, f_send.at[0], f_recv.at[0], x_next).start()
        send(c, c, xm_send.at[a], xm_recv.at[a], mate)

    def wait_xm(a):
        c = chunk(rel(a, -d), x + d + NX)
        remote(c, c, xm_send.at[a], xm_recv.at[a], mate).wait_recv()

    def step_f(f):
        c = chunk(far_chunk(f, core, d), x + 2)
        remote(c, c, f_send.at[f], f_recv.at[f], x_next).wait_recv()
        send(c, c, fm_send.at[f], fm_recv.at[f], mate)

    def wait_fm(f):
        c = chunk(far_chunk(f, 1 - core, -d), x + 2)
        remote(c, c, fm_send.at[f], fm_recv.at[f], mate).wait_recv()

    def tail_own():
        c = tail(z, x)
        send(c, c, q_send.at[0], q_recv.at[0], x_next)
        half = half_tail(z, x, core)
        send(half, half, q_send.at[1], q_recv.at[1], x_far)

    def tail_1():
        c = tail(z, x - d + NX)
        remote(c, c, q_send.at[0], q_recv.at[0], x_next).wait_recv()
        send(c, c, qm_send.at[0], qm_recv.at[0], mate)

    def tail_2():
        half = half_tail(z, x + 2, core)
        remote(half, half, q_send.at[1], q_recv.at[1], x_far).wait_recv()
        send(half, half, qm_send.at[1], qm_recv.at[1], mate)

    def t_copy(t, c):
        to = (z_next, z_next2, z_next, z_next2)[t]
        return remote(c, c, t_send.at[t], t_recv.at[t], to)

    def t_mate(t):
        c = tail_row(z - d * (t + 1) + NZ)
        return remote(c, c, tm_send.at[t], tm_recv.at[t], mate)

    def tail_3():
        c = tail(z, x + d + NX)
        remote(c, c, qm_send.at[0], qm_recv.at[0], mate).wait_recv()
        half = half_tail(z, x + 2, 1 - core)
        remote(half, half, qm_send.at[1], qm_recv.at[1], mate).wait_recv()
        for t in (1, 0):
            copy = t_copy(t, tail_row(z))
            copy.start()
            sent.append(copy)

    def step_tail(t):
        c = tail_row(z - d * (t + 1) + NZ)
        if t == FAR:
            @pl.when(even)
            def _():
                t_copy(t, c).wait_recv()
                t_mate(t).start()

            return
        t_copy(t, c).wait_recv()
        if t == 1:
            @pl.when(even)
            def _():
                t_copy(3, c).start()

            copy = t_copy(2, c)
            copy.start()
            sent.append(copy)
        copy = t_mate(t)
        copy.start()
        sent.append(copy)

    def wait_tm(t):
        c = tail_row(z + d * (t + 1) + NZ)
        copy = remote(c, c, tm_send.at[t], tm_recv.at[t], mate)
        if t == FAR:
            @pl.when(jnp.logical_not(even))
            def _():
                copy.wait_recv()
        else:
            copy.wait_recv()

    rate = (1.0 / math.sqrt(HD)) * math.log2(math.e)
    low = jnp.where(seq > 0, 3e38, -1e30).astype(jnp.float32)
    high = jnp.where(seq < SEQ - 1, 3e38, -1e30).astype(jnp.float32)

    def attend(h):
        cols = pl.ds(h * HD, HD)
        query = q_ref[:, cols]
        best = None
        for i in range(SLOTS):
            s = lax.dot_general(
                query, kbuf[i], (((1,), (1,)), ((), ())), preferred_element_type=jnp.float32
            )
            if i == 0:
                s = jnp.minimum(s, low)
            if i == 2:
                s = jnp.minimum(s, high)
            s_ref[:, i * BLK : (i + 1) * BLK] = s
            top = jnp.maximum(s[:, :HD], s[:, HD:])
            best = top if best is None else jnp.maximum(best, top)
        peak = jnp.max(best, axis=1, keepdims=True)
        total = jnp.zeros((BLK, HD), jnp.float32)
        blended = jnp.zeros((BLK, HD), jnp.float32)
        for i in range(SLOTS):
            w = jnp.exp2((s_ref[:, i * BLK : (i + 1) * BLK] - peak) * rate)
            total = total + w[:, :HD] + w[:, HD:]
            blended = blended + jnp.dot(
                w.astype(jnp.bfloat16), vbuf[i], preferred_element_type=jnp.float32
            )
        weight_sum = jnp.sum(total, axis=1, keepdims=True)
        att[0, :, cols] = (blended / weight_sum).astype(jnp.bfloat16)
        send(
            att.at[0, :, cols], att.at[1, :, cols], a_send.at[h], a_recv.at[h], seq, 1 - head
        )

    def wait_att(h):
        cols = pl.ds(h * HD, HD)
        remote(
            att.at[0, :, cols], att.at[1, :, cols], a_send.at[h], a_recv.at[h], seq, 1 - head
        ).wait_recv()

    def project(xx):
        xx = xx % NX
        part = None
        for side in range(2):
            w = wbuf[xx, side].reshape(HALF * PACK, ROWS)
            term = lax.dot_general(
                att[side], w, (((1,), (1,)), ((), ())), preferred_element_type=jnp.float32
            )
            part = term if part is None else part + term
        acc[xx] = part

    for i in range(NY * NC):
        remote(w_hbm, shards.at[i], sh_send.at[0], sh_recv.at[i], sh_to[0], head_to).wait_recv()
    own = whole(z, x)
    rows = [shards[i].astype(jnp.float32) for i in range(NY * NC)]
    own[...] = jnp.concatenate(rows, axis=0).astype(jnp.bfloat16)

    def wait_kv(i):
        remote(k_hbm, kbuf.at[i], kv_send.at[i, 0], kv_recv.at[i, 0], kv_to[i]).wait_recv()
        remote(v_hbm, vbuf.at[i], kv_send.at[i, 1], kv_recv.at[i, 1], kv_to[i]).wait_recv()

    tail_own()
    send_z(1)
    send_z(0)
    send_x(0)
    tail_1()
    tail_2()
    step_x(0)
    tail_3()
    hop_z(1)
    hop_z(0)
    side_z(1)
    side_z(0)
    for copy in loads:
        copy.wait()
    for i in order:
        wait_kv(i)
    attend(0)
    step_x(3)
    attend(1)
    step_x(1)
    attend(2)
    step_tail(1)
    step_x(4)
    attend(3)
    step_x(2)
    step_tail(0)
    attend(4)
    step_f(2)
    hop_z(3)
    attend(5)
    step_f(1)
    hop_z(2)
    side_z(3)
    attend(6)
    side_z(2)
    step_tail(3)
    step_tail(2)
    step_x(5)
    step_x(7)
    step_x(6)
    step_f(3)
    step_f(0)
    for t in range(FAR + 1):
        wait_tm(t)
    for h in range(QPK):
        wait_att(h)
    project(x)
    project(x - d + NX)
    for a in range(8):
        wait_xm(a)
    project(x + d + NX)
    for f in range(4):
        wait_fm(f)
    project(x + 2)
    for zz in range(HALF):
        for xx in range(NX):
            at_col = (zz * NX + xx) * PACK
            out_ref[:, at_col : at_col + PACK] = acc[
                xx, :, zz * PACK : (zz + 1) * PACK
            ].astype(jnp.bfloat16)

    for copy in sent:
        copy.wait_send()
    c = chunk(z + 4 * core, x - d + NX)
    remote(c, c, f_send.at[0], f_recv.at[0], x_next).wait_send()

    @pl.when(even)
    def _():
        far = chunk(z - 2 * d + NZ, x)
        z_copy(FAR, far).wait_send()
        z_mate(FAR).wait_send()
        t_copy(FAR, tail_row(z - 2 * d + NZ)).wait_send()
        t_mate(FAR).wait_send()

    @pl.when(jnp.logical_not(keep))
    def _():
        sh_self.wait_send()


def local(queries, key_rows, value_rows, out_weight):
    dma = pltpu.SemaphoreType.DMA
    f32, bf16 = jnp.float32, jnp.bfloat16
    shard_count = NY * NC
    return pl.pallas_call(
        body,
        out_shape=jax.ShapeDtypeStruct((BLK, HALF * NX * PACK), bf16),
        in_specs=[pl.BlockSpec(memory_space=pltpu.MemorySpace.HBM)] * 4,
        out_specs=pl.BlockSpec(memory_space=pltpu.VMEM),
        scratch_shapes=[
            pltpu.VMEM((BLK, ROWS), bf16),
            pltpu.VMEM((SLOTS, BLK, HD), bf16),
            pltpu.VMEM((SLOTS, BLK, HD), bf16),
            pltpu.VMEM((shard_count, SHARD, ROWS), bf16),
            pltpu.VMEM((NX, 2, HALF, PACK, ROWS), bf16),
            pltpu.VMEM((BLK, SLOTS * BLK), f32),
            pltpu.VMEM((2, BLK, ROWS), bf16),
            pltpu.VMEM((NX, BLK, HALF * PACK), f32),
            dma((3,)),
            dma((SLOTS, 2)), dma((SLOTS, 2)),
            dma((shard_count,)), dma((shard_count,)),
            dma((4,)), dma((4,)), dma((4,)), dma((4,)),
            dma((8,)), dma((8,)), dma((8,)), dma((8,)),
            dma((4,)), dma((4,)), dma((4,)), dma((4,)),
            dma((2,)), dma((2,)), dma((2,)), dma((2,)),
            dma((4,)), dma((4,)), dma((4,)), dma((4,)),
            dma((QPK,)), dma((QPK,)),
        ],
        compiler_params=pltpu.CompilerParams(
            collective_id=0, has_side_effects=True, vmem_limit_bytes=60 * 1024 * 1024
        ),
    )(queries, key_rows, value_rows, out_weight.T)


def solution(mesh):
    in_specs = (P("seq", "head"), P("seq", "head"), P("seq", "head"), P("head", "seq"))
    out_specs = P("seq", "head")
    return jax.shard_map(local, mesh=mesh, in_specs=in_specs, out_specs=out_specs, check_vma=False)
```

```python
import functools
import math

import jax
import jax.numpy as jnp
from jax import lax
from jax.experimental import pallas as pl
from jax.experimental.pallas import tpu as pltpu
from jax.sharding import PartitionSpec as P

QPK = 7
HD = 128
BLK = 256
MESH = pl.DeviceIdType.MESH
NZ, NX, NY, NC = 8, 4, 4, 2
HALF = NZ // 2
SEQ = NZ * NX * NY * NC
BITS = 8
SLOTS = BITS + 2
SHARD = 14
PACK = SHARD * NY * NC
ROWS = QPK * HD
FAR = 3
CUT = 6 * HD


def body(
    q_hbm, k_hbm, v_hbm, w_hbm, out_ref,
    q_ref, kbuf, vbuf, shards, wbuf, s_ref, att, acc,
    load_sem, kv_send, kv_recv, sh_send, sh_recv, shm_send, shm_recv, z_send, z_recv, zm_send, zm_recv,
    x_send, x_recv, xm_send, xm_recv, f_send, f_recv, fm_send, fm_recv,
    q_send, q_recv, qm_send, qm_recv, t_send, t_recv, tm_send, tm_recv, a_send, a_recv,
):
    seq = lax.axis_index("seq")
    head = lax.axis_index("head")
    core = seq % NC
    yh = (seq // NC) % NY
    x = (seq // (NC * NY)) % NX
    z = seq // (NC * NY * NX)
    d = 1 - 2 * core
    keep = (z // HALF + head) % 2 == 0

    def at(zz, xx, yy, cc):
        return ((zz % NZ * NX + xx % NX) * NY + yy % NY) * NC + cc % NC

    def flip(j):
        return seq + 2**j * (1 - 2 * ((seq // 2**j) % 2))

    kv_to = [(seq + 1) % SEQ, seq, (seq + SEQ - 1) % SEQ] + [flip(j) for j in range(1, BITS)]
    mate = at(z, x, yh, core + 1)
    x_next, x_prev = at(z, x + d + NX, yh, core), at(z, x - d + NX, yh, core)
    z_next, z_prev = at(z + d + NZ, x, yh, core), at(z - d + NZ, x, yh, core)
    z_next2, z_prev2 = at(z + 2 * d + NZ, x, yh, core), at(z - 2 * d + NZ, x, yh, core)
    x_far = at(z, x + 2, yh, core)

    away = (z // HALF + head) % 2
    z_to = z + away * (NZ - 1 - 2 * z)
    head_to = (head + away) % 2
    sh_to = [at(z_to, x, yh + i, core) for i in range(NY)]

    loads = [
        pltpu.make_async_copy(q_hbm, q_ref, load_sem.at[0]),
        pltpu.make_async_copy(k_hbm, kbuf.at[1], load_sem.at[1]),
        pltpu.make_async_copy(v_hbm, vbuf.at[1], load_sem.at[2]),
    ]
    for copy in loads:
        copy.start()

    barrier = pltpu.get_barrier_semaphore()

    def greet(s, h):
        pl.semaphore_signal(barrier, inc=1, device_id=(s, h), device_id_type=MESH)

    for i in range(SLOTS):
        if i != 1:
            greet(kv_to[i], head)
    for s in (x_next, x_prev, z_next, z_prev, z_next2, z_prev2):
        greet(s, head)
    greet(seq, 1 - head)
    for i in range(1, NY):
        greet(sh_to[i], head_to)

    @pl.when(jnp.logical_not(keep))
    def _():
        greet(sh_to[0], head_to)

    pl.semaphore_wait(barrier, SLOTS - 1 + 7 + NY - 1 + away)

    sent = []

    def remote(src, dst, send, recv, s, h=head):
        return pltpu.make_async_remote_copy(
            src_ref=src, dst_ref=dst, send_sem=send, recv_sem=recv, device_id=(s, h), device_id_type=MESH
        )

    def send(*args):
        copy = remote(*args)
        copy.start()
        sent.append(copy)

    mine = yh * NC + core
    sh_self = remote(w_hbm, shards.at[mine], sh_send.at[0], sh_recv.at[mine], sh_to[0], head_to)
    for i in range(1, NY):
        send(w_hbm, shards.at[mine], sh_send.at[i], sh_recv.at[mine], sh_to[i], head_to)

    @pl.when(keep)
    def _():
        pltpu.make_async_copy(w_hbm, shards.at[mine], sh_recv.at[mine]).start()

    @pl.when(jnp.logical_not(keep))
    def _():
        sh_self.start()

    order = [5, 6, 0, 2, 3, 4, 7, 8, 9]

    def send_kv(i):
        send(k_hbm, kbuf.at[i], kv_send.at[i, 0], kv_recv.at[i, 0], kv_to[i])
        send(v_hbm, vbuf.at[i], kv_send.at[i, 1], kv_recv.at[i, 1], kv_to[i])

    for i in order:
        send_kv(i)

    def place(zz):
        side = ((zz % NZ) // HALF + head) % 2
        quarter = zz % HALF
        return side, quarter + side * (HALF - 1 - 2 * quarter)

    def chunk(zz, xx):
        side, quarter = place(zz)
        return wbuf.at[xx % NX, side, quarter, :, pl.ds(0, CUT)]

    def whole(zz, xx):
        side, quarter = place(zz)
        return wbuf.at[xx % NX, side, quarter]

    def tail(zz, xx):
        side, quarter = place(zz)
        return wbuf.at[xx % NX, side, quarter, :, pl.ds(CUT, ROWS - CUT)]

    def tail_row(zz):
        side, quarter = place(zz)
        return wbuf.at[:, side, quarter, :, pl.ds(CUT, ROWS - CUT)]

    def rel(a, dd):
        return [0, -dd, dd, -2 * dd, 2 * dd, -3 * dd, 3 * dd, 4][a] + z + NZ

    even = z % 2 == core

    def z_copy(t, c):
        to = (z_next, z_next2, z_next, z_next2)[t]
        return remote(c, c, z_send.at[t], z_recv.at[t], to)

    def send_z(t):
        copy = z_copy(t, chunk(z, x))
        copy.start()
        sent.append(copy)

    def z_mate(t):
        c = chunk(z - d * (t + 1) + NZ, x)
        return remote(c, c, zm_send.at[t], zm_recv.at[t], mate)

    def hop_z(t):
        c = chunk(z - d * (t + 1) + NZ, x)
        if t == FAR:
            @pl.when(even)
            def _():
                z_copy(t, c).wait_recv()
                z_mate(t).start()

            return
        z_copy(t, c).wait_recv()
        if t == 1:
            @pl.when(even)
            def _():
                z_copy(3, c).start()

            copy = z_copy(2, c)
            copy.start()
            sent.append(copy)
        copy = z_mate(t)
        copy.start()
        sent.append(copy)
        send_x(2 * t + 1)

    def side_z(t):
        c = chunk(z + d * (t + 1) + NZ, x)
        copy = remote(c, c, zm_send.at[t], zm_recv.at[t], mate)
        if t == FAR:
            @pl.when(jnp.logical_not(even))
            def _():
                copy.wait_recv()

            send_x(7)
        else:
            copy.wait_recv()
            send_x(2 * t + 2)

    def send_x(a):
        c = chunk(rel(a, d), x)
        send(c, c, x_send.at[a], x_recv.at[a], x_next)

    def far_chunk(f, cc, dd):
        return z + 4 * cc if f == 0 else z - f * dd + NZ

    def step_x(a):
        c = chunk(rel(a, d), x - d + NX)
        remote(c, c, x_send.at[a], x_recv.at[a], x_next).wait_recv()
        if a in (1, 3, 5):
            f = (a + 1) // 2
            send(c, c, f_send.at[f], f_recv.at[f], x_next)
        if a in (0, 7):
            @pl.when(core == a // 7)
            def _():
                remote(c, c, f_send.at[0], f_recv.at[0], x_next).start()
        send(c, c, xm_send.at[a], xm_recv.at[a], mate)

    def wait_xm(a):
        c = chunk(rel(a, -d), x + d + NX)
        remote(c, c, xm_send.at[a], xm_recv.at[a], mate).wait_recv()

    def step_f(f):
        c = chunk(far_chunk(f, core, d), x + 2)
        remote(c, c, f_send.at[f], f_recv.at[f], x_next).wait_recv()
        send(c, c, fm_send.at[f], fm_recv.at[f], mate)

    def wait_fm(f):
        c = chunk(far_chunk(f, 1 - core, -d), x + 2)
        remote(c, c, fm_send.at[f], fm_recv.at[f], mate).wait_recv()

    def tail_own():
        c = tail(z, x)
        send(c, c, q_send.at[0], q_recv.at[0], x_next)
        send(c, c, q_send.at[1], q_recv.at[1], x_far)

    def tail_1():
        c = tail(z, x - d + NX)
        remote(c, c, q_send.at[0], q_recv.at[0], x_next).wait_recv()
        send(c, c, qm_send.at[0], qm_recv.at[0], mate)

    def tail_2():
        c = tail(z, x + 2)
        remote(c, c, q_send.at[1], q_recv.at[1], x_far).wait_recv()

    def t_copy(t, c):
        to = (z_next, z_next2, z_next, z_next2)[t]
        return remote(c, c, t_send.at[t], t_recv.at[t], to)

    def t_mate(t):
        c = tail_row(z - d * (t + 1) + NZ)
        return remote(c, c, tm_send.at[t], tm_recv.at[t], mate)

    def tail_3():
        c = tail(z, x + d + NX)
        remote(c, c, qm_send.at[0], qm_recv.at[0], mate).wait_recv()
        for t in (1, 0):
            copy = t_copy(t, tail_row(z))
            copy.start()
            sent.append(copy)

    def step_tail(t):
        c = tail_row(z - d * (t + 1) + NZ)
        if t == FAR:
            @pl.when(even)
            def _():
                t_copy(t, c).wait_recv()
                t_mate(t).start()

            return
        t_copy(t, c).wait_recv()
        if t == 1:
            @pl.when(even)
            def _():
                t_copy(3, c).start()

            copy = t_copy(2, c)
            copy.start()
            sent.append(copy)
        copy = t_mate(t)
        copy.start()
        sent.append(copy)

    def wait_tm(t):
        c = tail_row(z + d * (t + 1) + NZ)
        copy = remote(c, c, tm_send.at[t], tm_recv.at[t], mate)
        if t == FAR:
            @pl.when(jnp.logical_not(even))
            def _():
                copy.wait_recv()
        else:
            copy.wait_recv()

    rate = (1.0 / math.sqrt(HD)) * math.log2(math.e)
    low = jnp.where(seq > 0, 3e38, -1e30).astype(jnp.float32)
    high = jnp.where(seq < SEQ - 1, 3e38, -1e30).astype(jnp.float32)

    def attend(h):
        cols = pl.ds(h * HD, HD)
        query = q_ref[:, cols]
        best = None
        for i in range(SLOTS):
            s = lax.dot_general(
                query, kbuf[i], (((1,), (1,)), ((), ())), preferred_element_type=jnp.float32
            )
            if i == 0:
                s = jnp.minimum(s, low)
            if i == 2:
                s = jnp.minimum(s, high)
            s_ref[:, i * BLK : (i + 1) * BLK] = s
            top = jnp.maximum(s[:, :HD], s[:, HD:])
            best = top if best is None else jnp.maximum(best, top)
        peak = jnp.max(best, axis=1, keepdims=True)
        total = jnp.zeros((BLK, HD), jnp.float32)
        blended = jnp.zeros((BLK, HD), jnp.float32)
        for i in range(SLOTS):
            w = jnp.exp2((s_ref[:, i * BLK : (i + 1) * BLK] - peak) * rate)
            total = total + w[:, :HD] + w[:, HD:]
            blended = blended + jnp.dot(
                w.astype(jnp.bfloat16), vbuf[i], preferred_element_type=jnp.float32
            )
        weight_sum = jnp.sum(total, axis=1, keepdims=True)
        att[0, :, cols] = (blended / weight_sum).astype(jnp.bfloat16)
        send(
            att.at[0, :, cols], att.at[1, :, cols], a_send.at[h], a_recv.at[h], seq, 1 - head
        )

    def wait_att(h):
        cols = pl.ds(h * HD, HD)
        remote(
            att.at[0, :, cols], att.at[1, :, cols], a_send.at[h], a_recv.at[h], seq, 1 - head
        ).wait_recv()

    def project(xx):
        xx = xx % NX
        part = None
        for side in range(2):
            w = wbuf[xx, side].reshape(HALF * PACK, ROWS)
            term = lax.dot_general(
                att[side], w, (((1,), (1,)), ((), ())), preferred_element_type=jnp.float32
            )
            part = term if part is None else part + term
        acc[xx] = part

    for i in range(NY):
        c = shards.at[(yh + i) % NY * NC + core]
        remote(w_hbm, c, sh_send.at[0], sh_recv.at[(yh + i) % NY * NC + core], sh_to[0], head_to).wait_recv()
        send(c, c, shm_send.at[i], shm_recv.at[i], mate)
    for i in range(NY):
        c = shards.at[(yh + i) % NY * NC + 1 - core]
        remote(c, c, shm_send.at[i], shm_recv.at[i], mate).wait_recv()
    own = whole(z, x)
    rows = [shards[i].astype(jnp.float32) for i in range(NY * NC)]
    own[...] = jnp.concatenate(rows, axis=0).astype(jnp.bfloat16)

    def wait_kv(i):
        remote(k_hbm, kbuf.at[i], kv_send.at[i, 0], kv_recv.at[i, 0], kv_to[i]).wait_recv()
        remote(v_hbm, vbuf.at[i], kv_send.at[i, 1], kv_recv.at[i, 1], kv_to[i]).wait_recv()

    tail_own()
    send_z(1)
    send_z(0)
    send_x(0)
    tail_1()
    tail_2()
    tail_3()
    step_x(0)
    for copy in loads:
        copy.wait()
    for i in order:
        wait_kv(i)
    attend(0)
    hop_z(1)
    attend(1)
    hop_z(0)
    side_z(1)
    attend(2)
    side_z(0)
    attend(3)
    step_x(3)
    step_tail(1)
    step_tail(0)
    attend(4)
    step_x(1)
    attend(5)
    hop_z(3)
    step_x(4)
    attend(6)
    hop_z(2)
    side_z(3)
    step_x(2)
    step_tail(3)
    side_z(2)
    step_tail(2)
    step_f(2)
    step_f(1)
    step_x(5)
    step_x(7)
    step_x(6)
    step_f(3)
    step_f(0)
    for t in range(FAR + 1):
        wait_tm(t)
    for h in range(QPK):
        wait_att(h)
    project(x)
    project(x - d + NX)
    for a in range(8):
        wait_xm(a)
    project(x + d + NX)
    for f in range(4):
        wait_fm(f)
    project(x + 2)
    for zz in range(HALF):
        for xx in range(NX):
            at_col = (zz * NX + xx) * PACK
            out_ref[:, at_col : at_col + PACK] = acc[
                xx, :, zz * PACK : (zz + 1) * PACK
            ].astype(jnp.bfloat16)

    for copy in sent:
        copy.wait_send()
    c = chunk(z + 4 * core, x - d + NX)
    remote(c, c, f_send.at[0], f_recv.at[0], x_next).wait_send()

    @pl.when(even)
    def _():
        far = chunk(z - 2 * d + NZ, x)
        z_copy(FAR, far).wait_send()
        z_mate(FAR).wait_send()
        t_copy(FAR, tail_row(z - 2 * d + NZ)).wait_send()
        t_mate(FAR).wait_send()

    @pl.when(jnp.logical_not(keep))
    def _():
        sh_self.wait_send()


def local(queries, key_rows, value_rows, out_weight):
    dma = pltpu.SemaphoreType.DMA
    f32, bf16 = jnp.float32, jnp.bfloat16
    shard_count = NY * NC
    return pl.pallas_call(
        body,
        out_shape=jax.ShapeDtypeStruct((BLK, HALF * NX * PACK), bf16),
        in_specs=[pl.BlockSpec(memory_space=pltpu.MemorySpace.HBM)] * 4,
        out_specs=pl.BlockSpec(memory_space=pltpu.VMEM),
        scratch_shapes=[
            pltpu.VMEM((BLK, ROWS), bf16),
            pltpu.VMEM((SLOTS, BLK, HD), bf16),
            pltpu.VMEM((SLOTS, BLK, HD), bf16),
            pltpu.VMEM((shard_count, SHARD, ROWS), bf16),
            pltpu.VMEM((NX, 2, HALF, PACK, ROWS), bf16),
            pltpu.VMEM((BLK, SLOTS * BLK), f32),
            pltpu.VMEM((2, BLK, ROWS), bf16),
            pltpu.VMEM((NX, BLK, HALF * PACK), f32),
            dma((3,)),
            dma((SLOTS, 2)), dma((SLOTS, 2)),
            dma((NY,)), dma((shard_count,)), dma((NY,)), dma((NY,)),
            dma((4,)), dma((4,)), dma((4,)), dma((4,)),
            dma((8,)), dma((8,)), dma((8,)), dma((8,)),
            dma((4,)), dma((4,)), dma((4,)), dma((4,)),
            dma((2,)), dma((2,)), dma((1,)), dma((1,)),
            dma((4,)), dma((4,)), dma((4,)), dma((4,)),
            dma((QPK,)), dma((QPK,)),
        ],
        compiler_params=pltpu.CompilerParams(
            collective_id=0, has_side_effects=True, vmem_limit_bytes=60 * 1024 * 1024
        ),
    )(queries, key_rows, value_rows, out_weight.T)


def solution(mesh):
    in_specs = (P("seq", "head"), P("seq", "head"), P("seq", "head"), P("head", "seq"))
    out_specs = P("seq", "head")
    return jax.shard_map(local, mesh=mesh, in_specs=in_specs, out_specs=out_specs, check_vma=False)
```

```python
import functools
import math

import jax
import jax.numpy as jnp
from jax import lax
from jax.experimental import pallas as pl
from jax.experimental.pallas import tpu as pltpu
from jax.sharding import PartitionSpec as P

QPK = 7
HD = 128
BLK = 256
MESH = pl.DeviceIdType.MESH
NZ, NX, NY, NC = 8, 4, 4, 2
HALF = NZ // 2
SEQ = NZ * NX * NY * NC
BITS = 8
SLOTS = BITS + 2
SHARD = 14
PACK = SHARD * NY * NC
ROWS = QPK * HD
FAR = 3
CUT = 6 * HD


def body(
    q_hbm, k_hbm, v_hbm, w_hbm, out_ref,
    q_ref, kbuf, vbuf, shards, wbuf, s_ref, att, acc,
    load_sem, kv_send, kv_recv, sh_send, sh_recv, shm_send, shm_recv, z_send, z_recv, zm_send, zm_recv,
    x_send, x_recv, xm_send, xm_recv, f_send, f_recv, fm_send, fm_recv,
    q_send, q_recv, qm_send, qm_recv, t_send, t_recv, tm_send, tm_recv, a_send, a_recv,
):
    seq = lax.axis_index("seq")
    head = lax.axis_index("head")
    core = seq % NC
    yh = (seq // NC) % NY
    x = (seq // (NC * NY)) % NX
    z = seq // (NC * NY * NX)
    d = 1 - 2 * core
    keep = (z // HALF + head) % 2 == 0

    def at(zz, xx, yy, cc):
        return ((zz % NZ * NX + xx % NX) * NY + yy % NY) * NC + cc % NC

    def flip(j):
        return seq + 2**j * (1 - 2 * ((seq // 2**j) % 2))

    kv_to = [(seq + 1) % SEQ, seq, (seq + SEQ - 1) % SEQ] + [flip(j) for j in range(1, BITS)]
    mate = at(z, x, yh, core + 1)
    x_next, x_prev = at(z, x + d + NX, yh, core), at(z, x - d + NX, yh, core)
    z_next, z_prev = at(z + d + NZ, x, yh, core), at(z - d + NZ, x, yh, core)
    z_next2, z_prev2 = at(z + 2 * d + NZ, x, yh, core), at(z - 2 * d + NZ, x, yh, core)
    x_far = at(z, x + 2, yh, core)

    away = (z // HALF + head) % 2
    z_to = z + away * (NZ - 1 - 2 * z)
    head_to = (head + away) % 2
    sh_to = [at(z_to, x, yh + i, core) for i in range(NY)]

    loads = [
        pltpu.make_async_copy(q_hbm, q_ref, load_sem.at[0]),
        pltpu.make_async_copy(k_hbm, kbuf.at[1], load_sem.at[1]),
        pltpu.make_async_copy(v_hbm, vbuf.at[1], load_sem.at[2]),
    ]
    for copy in loads:
        copy.start()

    barrier = pltpu.get_barrier_semaphore()

    def greet(s, h):
        pl.semaphore_signal(barrier, inc=1, device_id=(s, h), device_id_type=MESH)

    for i in range(SLOTS):
        if i != 1:
            greet(kv_to[i], head)
    for s in (x_next, x_prev, z_next, z_prev, z_next2, z_prev2):
        greet(s, head)
    greet(seq, 1 - head)
    for i in range(1, NY):
        greet(sh_to[i], head_to)

    @pl.when(jnp.logical_not(keep))
    def _():
        greet(sh_to[0], head_to)

    pl.semaphore_wait(barrier, SLOTS - 1 + 7 + NY - 1 + away)

    sent = []

    def remote(src, dst, send, recv, s, h=head):
        return pltpu.make_async_remote_copy(
            src_ref=src, dst_ref=dst, send_sem=send, recv_sem=recv, device_id=(s, h), device_id_type=MESH
        )

    def send(*args):
        copy = remote(*args)
        copy.start()
        sent.append(copy)

    mine = yh * NC + core
    sh_self = remote(w_hbm, shards.at[mine], sh_send.at[0], sh_recv.at[mine], sh_to[0], head_to)
    for i in range(1, NY):
        send(w_hbm, shards.at[mine], sh_send.at[i], sh_recv.at[mine], sh_to[i], head_to)

    @pl.when(keep)
    def _():
        pltpu.make_async_copy(w_hbm, shards.at[mine], sh_recv.at[mine]).start()

    @pl.when(jnp.logical_not(keep))
    def _():
        sh_self.start()

    order = [5, 6, 0, 2, 3, 4, 7, 8, 9]

    def send_kv(i):
        send(k_hbm, kbuf.at[i], kv_send.at[i, 0], kv_recv.at[i, 0], kv_to[i])
        send(v_hbm, vbuf.at[i], kv_send.at[i, 1], kv_recv.at[i, 1], kv_to[i])

    for i in order:
        send_kv(i)

    def place(zz):
        side = ((zz % NZ) // HALF + head) % 2
        quarter = zz % HALF
        return side, quarter + side * (HALF - 1 - 2 * quarter)

    def chunk(zz, xx):
        side, quarter = place(zz)
        return wbuf.at[xx % NX, side, quarter, :, pl.ds(0, CUT)]

    def whole(zz, xx):
        side, quarter = place(zz)
        return wbuf.at[xx % NX, side, quarter]

    def tail(zz, xx):
        side, quarter = place(zz)
        return wbuf.at[xx % NX, side, quarter, :, pl.ds(CUT, ROWS - CUT)]

    def tail_row(zz):
        side, quarter = place(zz)
        return wbuf.at[:, side, quarter, :, pl.ds(CUT, ROWS - CUT)]

    def rel(a, dd):
        return [0, -dd, dd, -2 * dd, 2 * dd, -3 * dd, 3 * dd, 4][a] + z + NZ

    even = z % 2 == core

    def z_copy(t, c):
        to = (z_next, z_next2, z_next, z_next2)[t]
        return remote(c, c, z_send.at[t], z_recv.at[t], to)

    def send_z(t):
        copy = z_copy(t, chunk(z, x))
        copy.start()
        sent.append(copy)

    def z_mate(t):
        c = chunk(z - d * (t + 1) + NZ, x)
        return remote(c, c, zm_send.at[t], zm_recv.at[t], mate)

    def hop_z(t):
        c = chunk(z - d * (t + 1) + NZ, x)
        if t == FAR:
            @pl.when(even)
            def _():
                z_copy(t, c).wait_recv()
                z_mate(t).start()

            return
        z_copy(t, c).wait_recv()
        if t == 1:
            @pl.when(even)
            def _():
                z_copy(3, c).start()

            copy = z_copy(2, c)
            copy.start()
            sent.append(copy)
        copy = z_mate(t)
        copy.start()
        sent.append(copy)
        send_x(2 * t + 1)

    def side_z(t):
        c = chunk(z + d * (t + 1) + NZ, x)
        copy = remote(c, c, zm_send.at[t], zm_recv.at[t], mate)
        if t == FAR:
            @pl.when(jnp.logical_not(even))
            def _():
                copy.wait_recv()

            send_x(7)
        else:
            copy.wait_recv()
            send_x(2 * t + 2)

    def send_x(a):
        c = chunk(rel(a, d), x)
        send(c, c, x_send.at[a], x_recv.at[a], x_next)

    def far_chunk(f, cc, dd):
        return z + 4 * cc if f == 0 else z - f * dd + NZ

    def step_x(a):
        c = chunk(rel(a, d), x - d + NX)
        remote(c, c, x_send.at[a], x_recv.at[a], x_next).wait_recv()
        if a in (1, 3, 5):
            f = (a + 1) // 2
            send(c, c, f_send.at[f], f_recv.at[f], x_next)
        if a in (0, 7):
            @pl.when(core == a // 7)
            def _():
                remote(c, c, f_send.at[0], f_recv.at[0], x_next).start()
        send(c, c, xm_send.at[a], xm_recv.at[a], mate)

    def wait_xm(a):
        c = chunk(rel(a, -d), x + d + NX)
        remote(c, c, xm_send.at[a], xm_recv.at[a], mate).wait_recv()

    def step_f(f):
        c = chunk(far_chunk(f, core, d), x + 2)
        remote(c, c, f_send.at[f], f_recv.at[f], x_next).wait_recv()
        send(c, c, fm_send.at[f], fm_recv.at[f], mate)

    def wait_fm(f):
        c = chunk(far_chunk(f, 1 - core, -d), x + 2)
        remote(c, c, fm_send.at[f], fm_recv.at[f], mate).wait_recv()

    def tail_own():
        c = tail(z, x)
        send(c, c, q_send.at[0], q_recv.at[0], x_next)
        send(c, c, q_send.at[1], q_recv.at[1], x_far)

    def tail_1():
        c = tail(z, x - d + NX)
        remote(c, c, q_send.at[0], q_recv.at[0], x_next).wait_recv()
        send(c, c, qm_send.at[0], qm_recv.at[0], mate)

    def tail_2():
        c = tail(z, x + 2)
        remote(c, c, q_send.at[1], q_recv.at[1], x_far).wait_recv()

    def t_copy(t, c):
        to = (z_next, z_next2, z_next, z_next2)[t]
        return remote(c, c, t_send.at[t], t_recv.at[t], to)

    def t_mate(t):
        c = tail_row(z - d * (t + 1) + NZ)
        return remote(c, c, tm_send.at[t], tm_recv.at[t], mate)

    def tail_3():
        c = tail(z, x + d + NX)
        remote(c, c, qm_send.at[0], qm_recv.at[0], mate).wait_recv()
        for t in (1, 0):
            copy = t_copy(t, tail_row(z))
            copy.start()
            sent.append(copy)

    def step_tail(t):
        c = tail_row(z - d * (t + 1) + NZ)
        if t == FAR:
            @pl.when(even)
            def _():
                t_copy(t, c).wait_recv()
                t_mate(t).start()

            return
        t_copy(t, c).wait_recv()
        if t == 1:
            @pl.when(even)
            def _():
                t_copy(3, c).start()

            copy = t_copy(2, c)
            copy.start()
            sent.append(copy)
        copy = t_mate(t)
        copy.start()
        sent.append(copy)

    def wait_tm(t):
        c = tail_row(z + d * (t + 1) + NZ)
        copy = remote(c, c, tm_send.at[t], tm_recv.at[t], mate)
        if t == FAR:
            @pl.when(jnp.logical_not(even))
            def _():
                copy.wait_recv()
        else:
            copy.wait_recv()

    rate = (1.0 / math.sqrt(HD)) * math.log2(math.e)
    low = jnp.where(seq > 0, 3e38, -1e30).astype(jnp.float32)
    high = jnp.where(seq < SEQ - 1, 3e38, -1e30).astype(jnp.float32)

    def attend(h):
        cols = pl.ds(h * HD, HD)
        query = q_ref[:, cols]
        best = None
        for i in range(SLOTS):
            s = lax.dot_general(
                query, kbuf[i], (((1,), (1,)), ((), ())), preferred_element_type=jnp.float32
            )
            if i == 0:
                s = jnp.minimum(s, low)
            if i == 2:
                s = jnp.minimum(s, high)
            s_ref[:, i * BLK : (i + 1) * BLK] = s
            top = jnp.maximum(s[:, :HD], s[:, HD:])
            best = top if best is None else jnp.maximum(best, top)
        peak = jnp.max(best, axis=1, keepdims=True)
        total = jnp.zeros((BLK, HD), jnp.float32)
        blended = jnp.zeros((BLK, HD), jnp.float32)
        for i in range(SLOTS):
            w = jnp.exp2((s_ref[:, i * BLK : (i + 1) * BLK] - peak) * rate)
            total = total + w[:, :HD] + w[:, HD:]
            blended = blended + jnp.dot(
                w.astype(jnp.bfloat16), vbuf[i], preferred_element_type=jnp.float32
            )
        weight_sum = jnp.sum(total, axis=1, keepdims=True)
        att[0, :, cols] = (blended / weight_sum).astype(jnp.bfloat16)
        send(
            att.at[0, :, cols], att.at[1, :, cols], a_send.at[h], a_recv.at[h], seq, 1 - head
        )

    def wait_att(h):
        cols = pl.ds(h * HD, HD)
        remote(
            att.at[0, :, cols], att.at[1, :, cols], a_send.at[h], a_recv.at[h], seq, 1 - head
        ).wait_recv()

    def project(xx):
        xx = xx % NX
        part = None
        for side in range(2):
            w = wbuf[xx, side].reshape(HALF * PACK, ROWS)
            term = lax.dot_general(
                att[side], w, (((1,), (1,)), ((), ())), preferred_element_type=jnp.float32
            )
            part = term if part is None else part + term
        acc[xx] = part

    for i in range(NY):
        c = shards.at[(yh + i) % NY * NC + core]
        remote(w_hbm, c, sh_send.at[0], sh_recv.at[(yh + i) % NY * NC + core], sh_to[0], head_to).wait_recv()
        send(c, c, shm_send.at[i], shm_recv.at[i], mate)
    for i in range(NY):
        c = shards.at[(yh + i) % NY * NC + 1 - core]
        remote(c, c, shm_send.at[i], shm_recv.at[i], mate).wait_recv()
    own = whole(z, x)
    rows = [shards[i].astype(jnp.float32) for i in range(NY * NC)]
    own[...] = jnp.concatenate(rows, axis=0).astype(jnp.bfloat16)

    def wait_kv(i):
        remote(k_hbm, kbuf.at[i], kv_send.at[i, 0], kv_recv.at[i, 0], kv_to[i]).wait_recv()
        remote(v_hbm, vbuf.at[i], kv_send.at[i, 1], kv_recv.at[i, 1], kv_to[i]).wait_recv()

    tail_own()
    send_z(1)
    send_z(0)
    send_x(0)
    tail_1()
    tail_2()
    tail_3()
    step_x(0)
    hop_z(1)
    hop_z(0)
    side_z(1)
    side_z(0)
    for copy in loads:
        copy.wait()
    for i in order:
        wait_kv(i)
    attend(0)
    step_x(3)
    step_tail(1)
    step_tail(0)
    attend(1)
    step_x(1)
    attend(2)
    hop_z(3)
    step_x(4)
    attend(3)
    hop_z(2)
    step_x(2)
    side_z(3)
    attend(4)
    step_tail(3)
    step_tail(2)
    side_z(2)
    step_f(2)
    attend(5)
    step_f(1)
    attend(6)
    step_x(5)
    step_x(7)
    step_x(6)
    step_f(3)
    step_f(0)
    for t in range(FAR + 1):
        wait_tm(t)
    for h in range(QPK):
        wait_att(h)
    project(x)
    project(x - d + NX)
    for a in range(8):
        wait_xm(a)
    project(x + d + NX)
    for f in range(4):
        wait_fm(f)
    project(x + 2)
    for zz in range(HALF):
        for xx in range(NX):
            at_col = (zz * NX + xx) * PACK
            out_ref[:, at_col : at_col + PACK] = acc[
                xx, :, zz * PACK : (zz + 1) * PACK
            ].astype(jnp.bfloat16)

    for copy in sent:
        copy.wait_send()
    c = chunk(z + 4 * core, x - d + NX)
    remote(c, c, f_send.at[0], f_recv.at[0], x_next).wait_send()

    @pl.when(even)
    def _():
        far = chunk(z - 2 * d + NZ, x)
        z_copy(FAR, far).wait_send()
        z_mate(FAR).wait_send()
        t_copy(FAR, tail_row(z - 2 * d + NZ)).wait_send()
        t_mate(FAR).wait_send()

    @pl.when(jnp.logical_not(keep))
    def _():
        sh_self.wait_send()


def local(queries, key_rows, value_rows, out_weight):
    dma = pltpu.SemaphoreType.DMA
    f32, bf16 = jnp.float32, jnp.bfloat16
    shard_count = NY * NC
    return pl.pallas_call(
        body,
        out_shape=jax.ShapeDtypeStruct((BLK, HALF * NX * PACK), bf16),
        in_specs=[pl.BlockSpec(memory_space=pltpu.MemorySpace.HBM)] * 4,
        out_specs=pl.BlockSpec(memory_space=pltpu.VMEM),
        scratch_shapes=[
            pltpu.VMEM((BLK, ROWS), bf16),
            pltpu.VMEM((SLOTS, BLK, HD), bf16),
            pltpu.VMEM((SLOTS, BLK, HD), bf16),
            pltpu.VMEM((shard_count, SHARD, ROWS), bf16),
            pltpu.VMEM((NX, 2, HALF, PACK, ROWS), bf16),
            pltpu.VMEM((BLK, SLOTS * BLK), f32),
            pltpu.VMEM((2, BLK, ROWS), bf16),
            pltpu.VMEM((NX, BLK, HALF * PACK), f32),
            dma((3,)),
            dma((SLOTS, 2)), dma((SLOTS, 2)),
            dma((NY,)), dma((shard_count,)), dma((NY,)), dma((NY,)),
            dma((4,)), dma((4,)), dma((4,)), dma((4,)),
            dma((8,)), dma((8,)), dma((8,)), dma((8,)),
            dma((4,)), dma((4,)), dma((4,)), dma((4,)),
            dma((2,)), dma((2,)), dma((1,)), dma((1,)),
            dma((4,)), dma((4,)), dma((4,)), dma((4,)),
            dma((QPK,)), dma((QPK,)),
        ],
        compiler_params=pltpu.CompilerParams(
            collective_id=0, has_side_effects=True, vmem_limit_bytes=60 * 1024 * 1024
        ),
    )(queries, key_rows, value_rows, out_weight.T)


def solution(mesh):
    in_specs = (P("seq", "head"), P("seq", "head"), P("seq", "head"), P("head", "seq"))
    out_specs = P("seq", "head")
    return jax.shard_map(local, mesh=mesh, in_specs=in_specs, out_specs=out_specs, check_vma=False)
```
